32 devices in a mesh: ty: 2 (over y), tx: 4 (over x, core), ha: 4 (over z).
Axes of the slice: x: 2, y: 2, z: 4, core: 2. Of those that a mesh axis runs over, the one named last changes fastest.
Arguments:
- queries: bfloat16 [4, 16, 128, 5120], P(None, 'ty', 'tx', 'ha'), may hold values from -8 to 8
- keys_now: bfloat16 [4, 16, 128, 5120], P(None, 'ty', 'tx', 'ha'), may hold values from -8 to 8
- values_now: bfloat16 [4, 16, 128, 5120], P(None, 'ty', 'tx', 'ha'), may hold values from -6 to 6
- query_gain: float32 [5120], P('ha'), may hold values from 0.6 to 2
- key_gain: float32 [5120], P('ha'), may hold values from 0.6 to 2
- cached_keys: bfloat16 [512, 32, 5120], P(('ty', 'tx'), None, 'ha'), may hold values from -6 to 6
- cached_values: bfloat16 [512, 32, 5120], P(('ty', 'tx'), None, 'ha'), may hold values from -6 to 6
- block_lists: int32 [8, 48], P(('ty', 'tx')), may hold values from 0 to 511, as said below
- block_counts: int32 [8], P(('ty', 'tx')), may hold values from 6 to 48
Outputs:
- attended: bfloat16 [4, 16, 128, 5120], P(None, 'ty', 'tx', 'ha')
The draws below stay inside these ranges and needn't reach their ends.
Inputs may be any that keep to these rules, and one draw needn't show every extreme that they name: `block_lists`: each tile's 48 entries are distinct. The owner of id i is tile i // 64, tiles counted row by row over the tile grid. Of a tile's 48 entries, valid or not, at most 8 have the same owner, and some owner tile holds exactly 8 entries of every tile's list.
All inputs are finite; a program needn't handle non-finite values.
Results may differ from the reference program's by a relative error of at most 0.012.
The reference program's roundings to bfloat16 on the way count: a program that leaves them out, or rounds other values in their place, can miss the bound.
Values may be sent and summed in bfloat16 or wider, within the bound.
A program may use at most 128 MiB of HBM per device.

```python
import math
import jax
import jax.numpy as jnp
from jax import lax

HD = 128
FRAMES = 4
TH = 8
TW = 32
HALO = 4
NB = 48
HEADS = 40
FEAT = 5120
GH = 16
GW = 128
TOKB = 32
BPT = 64
TILES = 8
NBLK = 512
CAP = 8
N_TY = 2
N_TX = 4


def spread_field(key, salt_value):
    extent = (FRAMES, GH, GW, FEAT)
    column = jnp.arange(FEAT, dtype=jnp.float32)
    scramble = (jnp.arange(FEAT, dtype=jnp.int32) * 613 % 1009).astype(jnp.float32) / 1009.0
    baseline = jax.random.normal(jax.random.fold_in(key, salt_value), extent, jnp.float32)
    exponent = 0.3 * column / FEAT + 0.7 * scramble
    row_scale = jnp.exp(jax.random.uniform(jax.random.fold_in(key, salt_value + 1), (FRAMES, GH, GW, 1), jnp.float32, -1.2, 1.1))
    return baseline * 0.08 * jnp.power(10.0, exponent) * row_scale


def draw_queries(key, part):
    sampled = spread_field(key, 11)
    return jnp.clip(sampled, -8.0, 8.0).astype(jnp.bfloat16)


def draw_keys_now(key, part):
    sampled = spread_field(key, 21)
    return jnp.clip(sampled, -8.0, 8.0).astype(jnp.bfloat16)


def draw_block_lists(key, part):
    slot_total = TILES * CAP
    favourite = jax.random.randint(jax.random.fold_in(key, 5), (), 0, TILES)
    start_block = jax.random.randint(jax.random.fold_in(key, 6), (TILES, TILES), 0, BPT)
    slot_no = jnp.arange(slot_total, dtype=jnp.int32)
    slot_owner = slot_no // CAP
    slot_rank = slot_no % CAP

    def one_list(tile_no):
        tile_key = jax.random.fold_in(key, tile_no + 100)
        random_score = jax.random.randint(jax.random.fold_in(tile_key, 1), (slot_total,), 0, 262144)
        priority = jnp.where(slot_owner == favourite, slot_rank - CAP, random_score * slot_total + slot_no)
        picked = jnp.argsort(priority, stable=True)[:NB]
        shuffle_score = jax.random.randint(jax.random.fold_in(tile_key, 2), (NB,), 0, 262144) * NB + jnp.arange(NB, dtype=jnp.int32)
        shuffled = picked[jnp.argsort(shuffle_score, stable=True)]
        owner_list = slot_owner[shuffled]
        within = (start_block[tile_no, owner_list] + slot_rank[shuffled]) % BPT
        return (owner_list * BPT + within).astype(jnp.int32)
    return jax.vmap(one_list)(jnp.arange(TILES, dtype=jnp.int32))


def draw_block_counts(key, part):
    lower = NB // 8 + jax.random.randint(jax.random.fold_in(key, 31), (TILES,), 0, NB // 4 + 1)
    ranking = jax.random.permutation(jax.random.fold_in(key, 32), TILES)
    return jnp.where(ranking < max(1, TILES // 8), NB, lower).astype(jnp.int32)


def steps_of(rng, dims, cuts, low, largest):
    loudness, own = 1.0, jax.random.fold_in(rng, 6)
    for dim, blocks in cuts:
        heights = jnp.exp(jax.random.uniform(jax.random.fold_in(own, dim), (blocks,), jnp.float32, low / len(cuts), largest / len(cuts)))
        loudness = loudness * jnp.repeat(heights, dims[dim] // blocks).reshape([-1 if axis == dim else 1 for axis in range(len(dims))])
    return loudness


def gaussian(rng, shape, width, reach, cuts=(), kind=jnp.bfloat16):
    drawn = jax.random.normal(rng, shape, jnp.float32) * width
    if len(cuts) > 0:
        drawn = steps_of(rng, shape, cuts, -0.22, 0.18) * drawn
    return jnp.clip(drawn, min=-reach, max=reach).astype(kind)


def setup_inputs(seed: int = 0) -> dict:
    splits = jax.random.split(jax.random.key(seed), 10)
    return {
        "queries": draw_queries(jax.random.fold_in(splits[9], 71), 0),
        "keys_now": draw_keys_now(jax.random.fold_in(splits[9], 71), 0),
        "values_now": gaussian(splits[2], (FRAMES, GH, GW, FEAT), 1.0, 6.0, ((1, 2), (2, 4), (3, 4))),
        "query_gain": jnp.clip(jnp.exp(math.log(2.0) - 1.2039728 * jax.random.uniform(splits[3], (FEAT,), jnp.float32) ** steps_of(splits[3], (FEAT,), ((0, 4),), -0.2, 0.2)), 0.6, 2.0),
        "key_gain": jnp.clip(jnp.exp(math.log(2.0) - 1.2039728 * jax.random.uniform(splits[4], (FEAT,), jnp.float32) ** steps_of(splits[4], (FEAT,), ((0, 4),), -0.2, 0.2)), 0.6, 2.0),
        "cached_keys": gaussian(splits[5], (NBLK, TOKB, FEAT), 1.0, 6.0, ((0, 8), (2, 4))),
        "cached_values": gaussian(splits[6], (NBLK, TOKB, FEAT), 1.0, 6.0, ((0, 8), (2, 4))),
        "block_lists": draw_block_lists(jax.random.fold_in(splits[9], 71), 0),
        "block_counts": draw_block_counts(jax.random.fold_in(splits[9], 71), 0),
    }


epsilon = 1e-06
masked_score = -1e+30

def normed(values_in, gain_vector):
    widened = values_in.astype(jnp.float32)
    mean_square = lax.optimization_barrier(jnp.sum(widened * widened, axis=-1, keepdims=True)) / FEAT
    return (widened * lax.rsqrt(mean_square + epsilon) * gain_vector).astype(jnp.bfloat16)

def reference(queries, keys_now, values_now, query_gain, key_gain, cached_keys, cached_values, block_lists, block_counts):
    normed_query = lax.optimization_barrier(normed(queries, query_gain))
    normed_key = normed(keys_now, key_gain)
    margins = ((0, 0), (HALO, HALO), (HALO, HALO), (0, 0))
    key_padded = lax.optimization_barrier(jnp.pad(normed_key, margins))
    value_padded = jnp.pad(values_now, margins)
    span_rows = TH + 2 * HALO
    span_cols = TW + 2 * HALO
    query_frame = jnp.repeat(jnp.arange(FRAMES, dtype=jnp.int32), TH * TW)
    key_frame = jnp.repeat(jnp.arange(FRAMES, dtype=jnp.int32), span_rows * span_cols)
    scaling = HD ** (-0.5)

    def one_tile(tile_no):
        tile_row = tile_no // N_TX
        tile_col = tile_no % N_TX
        anchor = jnp.zeros((), jnp.int32)
        first_row = (tile_row * TH).astype(jnp.int32)
        first_col = (tile_col * TW).astype(jnp.int32)
        query_tile = lax.dynamic_slice(normed_query, (anchor, first_row, first_col, anchor), (FRAMES, TH, TW, FEAT))
        query_tile = query_tile.reshape(-1, HEADS, HD).astype(jnp.float32)
        key_tile = lax.dynamic_slice(key_padded, (anchor, first_row, first_col, anchor), (FRAMES, span_rows, span_cols, FEAT))
        key_tile = key_tile.reshape(-1, HEADS, HD).astype(jnp.float32)
        value_tile = lax.dynamic_slice(value_padded, (anchor, first_row, first_col, anchor), (FRAMES, span_rows, span_cols, FEAT))
        value_tile = value_tile.reshape(-1, HEADS, HD).astype(jnp.float32)
        grid_row = first_row - HALO + jnp.arange(span_rows, dtype=jnp.int32)
        grid_col = first_col - HALO + jnp.arange(span_cols, dtype=jnp.int32)
        inside = ((grid_row >= 0) & (grid_row < GH))[:, None] & ((grid_col >= 0) & (grid_col < GW))[None, :]
        inside = jnp.tile(inside.reshape(-1), FRAMES)
        visible = (key_frame[None, :] <= query_frame[:, None]) & inside[None, :]
        listed = block_lists[tile_no]
        far_keys = jnp.take(cached_keys, listed, axis=0).reshape(-1, HEADS, HD).astype(jnp.float32)
        far_values = jnp.take(cached_values, listed, axis=0).reshape(-1, HEADS, HD).astype(jnp.float32)
        usable = jnp.repeat(jnp.arange(NB, dtype=jnp.int32) < block_counts[tile_no], TOKB)
        near_scores = jnp.einsum('qhd,khd->hqk', query_tile, key_tile) * scaling
        near_scores = jnp.where(visible[None], near_scores, masked_score)
        far_scores = jnp.einsum('qhd,khd->hqk', query_tile, far_keys) * scaling
        far_scores = jnp.where(usable[None, None], far_scores, masked_score)
        row_max = jnp.maximum(lax.optimization_barrier(jnp.max(near_scores, axis=-1)), lax.optimization_barrier(jnp.max(far_scores, axis=-1)))
        near_exp = jnp.exp(near_scores - row_max[..., None])
        far_exp = jnp.exp(far_scores - row_max[..., None])
        totals = lax.optimization_barrier(jnp.sum(near_exp, axis=-1)) + lax.optimization_barrier(jnp.sum(far_exp, axis=-1))
        near_weights = lax.optimization_barrier(near_exp.astype(jnp.bfloat16)).astype(jnp.float32)
        far_weights = lax.optimization_barrier(far_exp.astype(jnp.bfloat16)).astype(jnp.float32)
        weighted = jnp.einsum('hqk,khd->hqd', near_weights, value_tile)
        weighted = weighted + jnp.einsum('hqk,khd->hqd', far_weights, far_values)
        result = (weighted / totals[..., None]).astype(jnp.bfloat16)
        return jnp.transpose(result, (1, 0, 2)).reshape(-1, FEAT)
    all_tiles = lax.map(one_tile, jnp.arange(TILES, dtype=jnp.int32))
    all_tiles = all_tiles.reshape(N_TY, N_TX, FRAMES, TH, TW, FEAT)
    return jnp.transpose(all_tiles, (2, 0, 3, 1, 4, 5)).reshape(FRAMES, GH, GW, FEAT)
```

```python
import functools
import math

import jax
import jax.numpy as jnp
from jax import lax
from jax.experimental import pallas as pl
from jax.experimental.pallas import tpu as pltpu
from jax.sharding import PartitionSpec as P

HD = 128
HALO = 4
CHUNK = 16

epsilon = 1e-06
masked_score = -1e30
log2_scale = HD ** (-0.5) * math.log2(math.e)


def neighbours(cells, axis, dim, width):
    count = lax.axis_size(axis)
    size = cells.shape[dim]
    head = lax.slice_in_dim(cells, 0, width, axis=dim)
    tail = lax.slice_in_dim(cells, size - width, size, axis=dim)
    where_am_i = lax.axis_index(axis)
    if count == 2:
        mine = jnp.where(where_am_i == 0, tail, head)
        got = lax.ppermute(mine, axis, [(0, 1), (1, 0)])
        return [(got, jnp.bool_(True))]
    ends = count - 1
    before = lax.ppermute(tail, axis, [(i, i + 1) for i in range(ends)])
    after = lax.ppermute(head, axis, [(i + 1, i) for i in range(ends)])
    return [(before, where_am_i > 0), (after, where_am_i < ends)]


def slot_ranks(owners):
    length = owners.shape[-1]
    earlier = lax.broadcasted_iota(jnp.int32, (length, length), 1) < lax.broadcasted_iota(
        jnp.int32, (length, length), 0
    )
    same_owner = owners[..., :, None] == owners[..., None, :]
    return jnp.sum(jnp.where(same_owner & earlier, 1, 0), axis=-1).astype(jnp.int32)


def near_kernel(frames, per_query, n_parts, q_ref, bias_ref, *refs):
    parts_k = refs[:n_parts]
    parts_v = refs[n_parts : 2 * n_parts]
    acc_ref, ml_ref, kbuf, vbuf = refs[2 * n_parts :]
    span = kbuf.shape[0] // frames
    for f in range(frames):
        start = f * span
        for k_ref, v_ref in zip(parts_k, parts_v):
            rows = k_ref.shape[1]
            kbuf[start : start + rows, :] = k_ref[f]
            vbuf[start : start + rows, :HD] = v_ref[f]
            start += rows
    vbuf[:, HD:] = jnp.ones((vbuf.shape[0], HD), jnp.bfloat16)
    for f in range(frames):
        keys = (f + 1) * span
        s = lax.dot_general(
            q_ref[f], kbuf[:keys], (((1,), (1,)), ((), ())), preferred_element_type=jnp.float32
        )
        s = s + bias_ref[:, :keys]
        m = jnp.max(s, axis=1, keepdims=True) * log2_scale
        p = jnp.exp2(s * log2_scale - m).astype(jnp.bfloat16)
        o = jnp.dot(p, vbuf[:keys], preferred_element_type=jnp.float32)
        acc_ref[f] = o[:, :HD]
        lane = lax.broadcasted_iota(jnp.int32, (per_query, HD), 1)
        ml_ref[0, f] = jnp.where(lane < HD // 2, m, o[:, HD:])


def far_kernel(
    frames, per_query, tokens, count_ref, slot_ref, q_ref, acc_in, ml_in, k_ref, v_ref, out_ref,
    kbuf, vbuf, m_sc, l_sc, acc_sc,
):
    count = count_ref[0]
    vbuf[:, HD:] = jnp.ones((vbuf.shape[0], HD), jnp.bfloat16)
    for f in range(frames):
        ml = ml_in[0, f]
        m_sc[f] = jnp.broadcast_to(ml[:, :1], (per_query, HD))
        l_sc[f] = jnp.broadcast_to(ml[:, HD // 2 : HD // 2 + 1], (per_query, HD))
        acc_sc[f] = acc_in[f]

    def chunk(c, carry):
        for i in range(CHUNK):
            slot = slot_ref[c * CHUNK + i]
            kbuf[i * tokens : (i + 1) * tokens, :] = k_ref[slot]
            vbuf[i * tokens : (i + 1) * tokens, :HD] = v_ref[slot]
        place = lax.broadcasted_iota(jnp.int32, (1, CHUNK * tokens), 1)
        bias = jnp.where(place < (count - c * CHUNK) * tokens, 0.0, masked_score)
        for f in range(frames):
            s = lax.dot_general(
                q_ref[f], kbuf[...], (((1,), (1,)), ((), ())), preferred_element_type=jnp.float32
            )
            s = s + bias
            m_old = m_sc[f]
            m_new = jnp.maximum(m_old, jnp.max(s, axis=1, keepdims=True) * log2_scale)
            p = jnp.exp2(s * log2_scale - m_new[:, :1]).astype(jnp.bfloat16)
            o = jnp.dot(p, vbuf[...], preferred_element_type=jnp.float32)
            a = jnp.exp2(m_old - m_new)
            acc_sc[f] = acc_sc[f] * a + o[:, :HD]
            l_sc[f] = l_sc[f] * a + o[:, HD:]
            m_sc[f] = m_new
        return carry

    lax.fori_loop(0, (count + CHUNK - 1) // CHUNK, chunk, 0)
    for f in range(frames):
        out_ref[f] = (acc_sc[f] / l_sc[f]).astype(jnp.bfloat16)


def near_attention(query, parts_k, parts_v, bias):
    frames, per_query, features = query.shape
    heads = features // HD
    span = sum(part.shape[1] for part in parts_k)

    def spec(rows):
        return pl.BlockSpec((frames, rows, HD), lambda h: (0, 0, h))

    part_specs = [spec(part.shape[1]) for part in parts_k]
    keys = frames * span
    return pl.pallas_call(
        functools.partial(near_kernel, frames, per_query, len(parts_k)),
        grid=(heads,),
        in_specs=[spec(per_query), pl.BlockSpec((1, keys), lambda h: (0, 0))]
        + part_specs
        + part_specs,
        out_specs=[
            spec(per_query),
            pl.BlockSpec((1, frames, per_query, HD), lambda h: (h, 0, 0, 0)),
        ],
        out_shape=[
            jax.ShapeDtypeStruct((frames, per_query, features), jnp.float32),
            jax.ShapeDtypeStruct((heads, frames, per_query, HD), jnp.float32),
        ],
        scratch_shapes=[
            pltpu.VMEM((keys, HD), jnp.bfloat16),
            pltpu.VMEM((keys, 2 * HD), jnp.bfloat16),
        ],
        compiler_params=pltpu.CompilerParams(vmem_limit_bytes=40 << 20),
        cost_estimate=pl.CostEstimate(
            flops=heads * frames * per_query * keys * HD * 6,
            bytes_accessed=30 << 20,
            transcendentals=heads * frames * per_query * keys,
        ),
        name="near",
    )(query, bias, *parts_k, *parts_v)


def far_attention(query, acc, ml, keys, values, count, slots, head0):
    frames, per_query, features = query.shape
    all_slots, tokens, width = keys.shape
    heads = width // HD
    spec = pl.BlockSpec((frames, per_query, HD), lambda h, *_: (0, 0, h + head0))
    block = pl.BlockSpec((all_slots, tokens, HD), lambda h, *_: (0, 0, h))
    return pl.pallas_call(
        functools.partial(far_kernel, frames, per_query, tokens),
        grid_spec=pltpu.PrefetchScalarGridSpec(
            num_scalar_prefetch=2,
            grid=(heads,),
            in_specs=[
                spec,
                spec,
                pl.BlockSpec((1, frames, per_query, HD), lambda h, *_: (h + head0, 0, 0, 0)),
                block,
                block,
            ],
            out_specs=pl.BlockSpec((frames, per_query, HD), lambda h, *_: (0, 0, h)),
            scratch_shapes=[
                pltpu.VMEM((CHUNK * tokens, HD), jnp.bfloat16),
                pltpu.VMEM((CHUNK * tokens, 2 * HD), jnp.bfloat16),
                pltpu.VMEM((frames, per_query, HD), jnp.float32),
                pltpu.VMEM((frames, per_query, HD), jnp.float32),
                pltpu.VMEM((frames, per_query, HD), jnp.float32),
            ],
        ),
        out_shape=jax.ShapeDtypeStruct((frames, per_query, width), jnp.bfloat16),
        compiler_params=pltpu.CompilerParams(vmem_limit_bytes=40 << 20),
        cost_estimate=pl.CostEstimate(
            flops=heads * frames * per_query * 1536 * HD * 6,
            bytes_accessed=30 << 20,
            transcendentals=heads * frames * per_query * 1536,
        ),
        name="far",
    )(count, slots, query, acc, ml, keys, values)


def local(
    queries,
    keys_now,
    values_now,
    query_gain,
    key_gain,
    cached_keys,
    cached_values,
    block_lists,
    block_counts,
):
    frames, tile_rows, tile_cols, features = queries.shape
    owners_all = lax.axis_size("ty") * lax.axis_size("tx")
    full_width = features * lax.axis_size("ha")
    per_query = tile_rows * tile_cols
    per_tile, block_tokens = cached_keys.shape[:2]

    listed = block_lists[0]
    list_length = listed.shape[0]
    owners = listed // per_tile
    within = listed % per_tile
    slot_rank = slot_ranks(owners)
    capacity = max(2, 4 * list_length // (3 * owners_all))
    target = owners * capacity + slot_rank
    all_slots = lax.broadcasted_iota(jnp.int32, (1, owners_all * capacity), 1)
    matches = target[:, None] == all_slots
    outgoing = jnp.sum(jnp.where(matches, within[:, None], 0), axis=0).reshape(owners_all, capacity)
    wanted = lax.all_to_all(outgoing, ("ty", "tx"), split_axis=0, concat_axis=0, tiled=True)
    wanted = wanted.reshape(-1)

    def fetch(cached):
        out = cached.at[wanted].get(mode="promise_in_bounds")
        out = out.reshape(owners_all, capacity, block_tokens, features)
        back = lax.all_to_all(out, ("ty", "tx"), split_axis=0, concat_axis=0, tiled=True)
        return back.reshape(owners_all * capacity, block_tokens, features)

    far_keys = fetch(cached_keys)
    far_values = fetch(cached_values)

    query_wide = queries.astype(jnp.float32)
    key_wide = keys_now.astype(jnp.float32)
    query_sq, key_sq = lax.psum(
        (jnp.sum(query_wide * query_wide, axis=-1), jnp.sum(key_wide * key_wide, axis=-1)), "ha"
    )
    normed_key = (key_wide * lax.rsqrt(key_sq / full_width + epsilon)[..., None] * key_gain).astype(
        jnp.bfloat16
    )
    normed_query = (
        query_wide * lax.rsqrt(query_sq / full_width + epsilon)[..., None] * query_gain
    ).astype(jnp.bfloat16)

    paired = jnp.stack([normed_key, values_now])
    row_parts = neighbours(paired, "ty", 2, HALO)
    column = jnp.concatenate(
        [jnp.concatenate([part[..., :HALO, :], part[..., -HALO:, :]], axis=3) for part in
         [paired] + [got for got, _ in row_parts]],
        axis=2,
    )
    tall = column.shape[2]
    ok_rows = [jnp.ones((tile_rows,), bool)] + [
        jnp.broadcast_to(ok, (HALO,)) for _, ok in row_parts
    ]
    ok_rows = jnp.concatenate(ok_rows)
    column_parts = neighbours(column, "tx", 3, HALO)

    pieces = [paired.reshape(2, frames, -1, features)]
    oks = [jnp.ones((per_query,), bool)]
    for got, ok in row_parts:
        pieces.append(got.reshape(2, frames, -1, features))
        oks.append(jnp.broadcast_to(ok, (HALO * tile_cols,)))
    for got, ok in column_parts:
        pieces.append(got.reshape(2, frames, -1, features))
        oks.append(jnp.repeat(ok_rows & ok, HALO))
    bias = jnp.where(jnp.concatenate(oks), 0.0, masked_score).astype(jnp.float32)
    bias = jnp.tile(bias, frames)[None]
    parts_k = [normed_key.reshape(frames, -1, features)] + [piece[0] for piece in pieces[1:]]
    parts_v = [values_now.reshape(frames, -1, features)] + [piece[1] for piece in pieces[1:]]

    flat_query = normed_query.reshape(frames, per_query, features)
    acc, ml = near_attention(flat_query, parts_k, parts_v, bias)
    padding = (-list_length) % CHUNK
    slots = jnp.pad(target, (0, padding))
    attended = far_attention(flat_query, acc, ml, far_keys, far_values, block_counts, slots, 0)
    return attended.reshape(frames, tile_rows, tile_cols, features)


def solution(mesh):
    return jax.shard_map(
        local,
        mesh=mesh,
        in_specs=(
            P(None, "ty", "tx", "ha"),
            P(None, "ty", "tx", "ha"),
            P(None, "ty", "tx", "ha"),
            P("ha"),
            P("ha"),
            P(("ty", "tx"), None, "ha"),
            P(("ty", "tx"), None, "ha"),
            P(("ty", "tx"), None),
            P(("ty", "tx")),
        ),
        out_specs=P(None, "ty", "tx", "ha"),
        check_vma=False,
    )
```

```python
import functools
import math

import jax
import jax.numpy as jnp
from jax import lax
from jax.experimental import pallas as pl
from jax.experimental.pallas import tpu as pltpu
from jax.sharding import PartitionSpec as P

HD = 128
HALO = 4
CHUNK = 16

epsilon = 1e-06
masked_score = -1e30
log2_scale = HD ** (-0.5) * math.log2(math.e)


def neighbours(cells, axis, dim, width):
    count = lax.axis_size(axis)
    size = cells.shape[dim]
    head = lax.slice_in_dim(cells, 0, width, axis=dim)
    tail = lax.slice_in_dim(cells, size - width, size, axis=dim)
    where_am_i = lax.axis_index(axis)
    if count == 2:
        mine = jnp.where(where_am_i == 0, tail, head)
        got = lax.ppermute(mine, axis, [(0, 1), (1, 0)])
        return [(got, jnp.bool_(True))]
    ends = count - 1
    before = lax.ppermute(tail, axis, [(i, i + 1) for i in range(ends)])
    after = lax.ppermute(head, axis, [(i + 1, i) for i in range(ends)])
    return [(before, where_am_i > 0), (after, where_am_i < ends)]


def slot_ranks(owners):
    length = owners.shape[-1]
    earlier = lax.broadcasted_iota(jnp.int32, (length, length), 1) < lax.broadcasted_iota(
        jnp.int32, (length, length), 0
    )
    same_owner = owners[..., :, None] == owners[..., None, :]
    return jnp.sum(jnp.where(same_owner & earlier, 1, 0), axis=-1).astype(jnp.int32)


def near_kernel(frames, per_query, n_parts, q_ref, bias_ref, *refs):
    parts_k = refs[:n_parts]
    parts_v = refs[n_parts : 2 * n_parts]
    acc_ref, ml_ref, kbuf, vbuf = refs[2 * n_parts :]
    span = kbuf.shape[0] // frames
    for f in range(frames):
        start = f * span
        for k_ref, v_ref in zip(parts_k, parts_v):
            rows = k_ref.shape[1]
            kbuf[start : start + rows, :] = k_ref[f]
            vbuf[start : start + rows, :HD] = v_ref[f]
            start += rows
    vbuf[:, HD:] = jnp.ones((vbuf.shape[0], HD), jnp.bfloat16)
    for f in range(frames):
        keys = (f + 1) * span
        s = lax.dot_general(
            q_ref[f], kbuf[:keys], (((1,), (1,)), ((), ())), preferred_element_type=jnp.float32
        )
        s = s + bias_ref[:, :keys]
        m = jnp.max(s, axis=1, keepdims=True) * log2_scale
        p = jnp.exp2(s * log2_scale - m).astype(jnp.bfloat16)
        o = jnp.dot(p, vbuf[:keys], preferred_element_type=jnp.float32)
        acc_ref[f] = o[:, :HD]
        lane = lax.broadcasted_iota(jnp.int32, (per_query, HD), 1)
        ml_ref[0, f] = jnp.where(lane < HD // 2, m, o[:, HD:])


def far_kernel(
    frames, per_query, tokens, count_ref, slot_ref, q_ref, acc_in, ml_in, k_ref, v_ref, out_ref,
    kbuf, vbuf, m_sc, l_sc, acc_sc,
):
    count = count_ref[0]
    vbuf[:, HD:] = jnp.ones((vbuf.shape[0], HD), jnp.bfloat16)
    for f in range(frames):
        ml = ml_in[0, f]
        m_sc[f] = jnp.broadcast_to(ml[:, :1], (per_query, HD))
        l_sc[f] = jnp.broadcast_to(ml[:, HD // 2 : HD // 2 + 1], (per_query, HD))
        acc_sc[f] = acc_in[f]

    def chunk(c, carry):
        for i in range(CHUNK):
            slot = slot_ref[c * CHUNK + i]
            kbuf[i * tokens : (i + 1) * tokens, :] = k_ref[slot, 0]
            vbuf[i * tokens : (i + 1) * tokens, :HD] = v_ref[slot, 0]
        place = lax.broadcasted_iota(jnp.int32, (1, CHUNK * tokens), 1)
        bias = jnp.where(place < (count - c * CHUNK) * tokens, 0.0, masked_score)
        for f in range(frames):
            s = lax.dot_general(
                q_ref[f], kbuf[...], (((1,), (1,)), ((), ())), preferred_element_type=jnp.float32
            )
            s = s + bias
            m_old = m_sc[f]
            m_new = jnp.maximum(m_old, jnp.max(s, axis=1, keepdims=True) * log2_scale)
            p = jnp.exp2(s * log2_scale - m_new[:, :1]).astype(jnp.bfloat16)
            o = jnp.dot(p, vbuf[...], preferred_element_type=jnp.float32)
            a = jnp.exp2(m_old - m_new)
            acc_sc[f] = acc_sc[f] * a + o[:, :HD]
            l_sc[f] = l_sc[f] * a + o[:, HD:]
            m_sc[f] = m_new
        return carry

    lax.fori_loop(0, (count + CHUNK - 1) // CHUNK, chunk, 0)
    for f in range(frames):
        out_ref[f] = (acc_sc[f] / l_sc[f]).astype(jnp.bfloat16)


def near_attention(query, parts_k, parts_v, bias):
    frames, per_query, features = query.shape
    heads = features // HD
    span = sum(part.shape[1] for part in parts_k)

    def spec(rows):
        return pl.BlockSpec((frames, rows, HD), lambda h: (0, 0, h))

    part_specs = [spec(part.shape[1]) for part in parts_k]
    keys = frames * span
    return pl.pallas_call(
        functools.partial(near_kernel, frames, per_query, len(parts_k)),
        grid=(heads,),
        in_specs=[spec(per_query), pl.BlockSpec((1, keys), lambda h: (0, 0))]
        + part_specs
        + part_specs,
        out_specs=[
            spec(per_query),
            pl.BlockSpec((1, frames, per_query, HD), lambda h: (h, 0, 0, 0)),
        ],
        out_shape=[
            jax.ShapeDtypeStruct((frames, per_query, features), jnp.float32),
            jax.ShapeDtypeStruct((heads, frames, per_query, HD), jnp.float32),
        ],
        scratch_shapes=[
            pltpu.VMEM((keys, HD), jnp.bfloat16),
            pltpu.VMEM((keys, 2 * HD), jnp.bfloat16),
        ],
        compiler_params=pltpu.CompilerParams(vmem_limit_bytes=40 << 20),
        cost_estimate=pl.CostEstimate(
            flops=heads * frames * per_query * keys * HD * 6,
            bytes_accessed=30 << 20,
            transcendentals=heads * frames * per_query * keys,
        ),
        name="near",
    )(query, bias, *parts_k, *parts_v)


def pick_kernel(total, wanted_ref, keys_ref, values_ref, out_ref, sem):
    def send(i, carry):
        block = wanted_ref[i]
        pltpu.make_async_copy(keys_ref.at[block], out_ref.at[i, 0], sem).start()
        pltpu.make_async_copy(values_ref.at[block], out_ref.at[i, 1], sem).start()
        return carry

    lax.fori_loop(0, total, send, 0)
    pltpu.make_async_copy(out_ref, out_ref, sem).wait()


def pick_blocks(wanted, keys, values):
    total = wanted.shape[0]
    return pl.pallas_call(
        functools.partial(pick_kernel, total),
        grid_spec=pltpu.PrefetchScalarGridSpec(
            num_scalar_prefetch=1,
            grid=(),
            in_specs=[pl.BlockSpec(memory_space=pl.ANY)] * 2,
            out_specs=pl.BlockSpec(memory_space=pl.ANY),
            scratch_shapes=[pltpu.SemaphoreType.DMA],
        ),
        out_shape=jax.ShapeDtypeStruct((total, 2) + keys.shape[1:], keys.dtype),
        cost_estimate=pl.CostEstimate(flops=0, bytes_accessed=20 << 20, transcendentals=0),
        name="pick",
    )(wanted, keys, values)


def far_attention(query, acc, ml, blocks, count, slots):
    frames, per_query, features = query.shape
    all_slots, _, tokens, width = blocks.shape
    heads = width // HD
    spec = pl.BlockSpec((frames, per_query, HD), lambda h, *_: (0, 0, h))
    k_spec = pl.BlockSpec((all_slots, 1, tokens, HD), lambda h, *_: (0, 0, 0, h))
    v_spec = pl.BlockSpec((all_slots, 1, tokens, HD), lambda h, *_: (0, 1, 0, h))
    return pl.pallas_call(
        functools.partial(far_kernel, frames, per_query, tokens),
        grid_spec=pltpu.PrefetchScalarGridSpec(
            num_scalar_prefetch=2,
            grid=(heads,),
            in_specs=[
                spec,
                spec,
                pl.BlockSpec((1, frames, per_query, HD), lambda h, *_: (h, 0, 0, 0)),
                k_spec,
                v_spec,
            ],
            out_specs=pl.BlockSpec((frames, per_query, HD), lambda h, *_: (0, 0, h)),
            scratch_shapes=[
                pltpu.VMEM((CHUNK * tokens, HD), jnp.bfloat16),
                pltpu.VMEM((CHUNK * tokens, 2 * HD), jnp.bfloat16),
                pltpu.VMEM((frames, per_query, HD), jnp.float32),
                pltpu.VMEM((frames, per_query, HD), jnp.float32),
                pltpu.VMEM((frames, per_query, HD), jnp.float32),
            ],
        ),
        out_shape=jax.ShapeDtypeStruct((frames, per_query, width), jnp.bfloat16),
        compiler_params=pltpu.CompilerParams(vmem_limit_bytes=40 << 20),
        cost_estimate=pl.CostEstimate(
            flops=heads * frames * per_query * 1536 * HD * 6,
            bytes_accessed=30 << 20,
            transcendentals=heads * frames * per_query * 1536,
        ),
        name="far",
    )(count, slots, query, acc, ml, blocks, blocks)


def local(
    queries,
    keys_now,
    values_now,
    query_gain,
    key_gain,
    cached_keys,
    cached_values,
    block_lists,
    block_counts,
):
    frames, tile_rows, tile_cols, features = queries.shape
    owners_all = lax.axis_size("ty") * lax.axis_size("tx")
    full_width = features * lax.axis_size("ha")
    per_query = tile_rows * tile_cols
    per_tile, block_tokens = cached_keys.shape[:2]

    listed = block_lists[0]
    list_length = listed.shape[0]
    owners = listed // per_tile
    within = listed % per_tile
    slot_rank = slot_ranks(owners)
    capacity = max(2, 4 * list_length // (3 * owners_all))
    target = owners * capacity + slot_rank
    all_slots = lax.broadcasted_iota(jnp.int32, (1, owners_all * capacity), 1)
    matches = target[:, None] == all_slots
    outgoing = jnp.sum(jnp.where(matches, within[:, None], 0), axis=0).reshape(owners_all, capacity)
    wanted = lax.all_to_all(outgoing, ("ty", "tx"), split_axis=0, concat_axis=0, tiled=True)
    wanted = wanted.reshape(-1)

    out = pick_blocks(wanted, cached_keys, cached_values)
    back = lax.all_to_all(
        out.reshape((owners_all, capacity) + out.shape[1:]),
        ("ty", "tx"),
        split_axis=0,
        concat_axis=0,
        tiled=True,
    )
    far_blocks = back.reshape((-1,) + out.shape[1:])

    paired = jnp.stack([keys_now, values_now])
    row_parts = neighbours(paired, "ty", 2, HALO)
    column = jnp.concatenate(
        [jnp.concatenate([part[..., :HALO, :], part[..., -HALO:, :]], axis=3) for part in
         [paired] + [got for got, _ in row_parts]],
        axis=2,
    )
    column_parts = neighbours(column, "tx", 3, HALO)

    query_wide = queries.astype(jnp.float32)
    key_wide = keys_now.astype(jnp.float32)
    query_sq, key_sq = lax.psum(
        (jnp.sum(query_wide * query_wide, axis=-1), jnp.sum(key_wide * key_wide, axis=-1)), "ha"
    )

    def normed(wide, squares, gain):
        return (wide * lax.rsqrt(squares / full_width + epsilon)[..., None] * gain).astype(
            jnp.bfloat16
        )

    normed_key = normed(key_wide, key_sq, key_gain)
    normed_query = normed(query_wide, query_sq, query_gain)

    ok_rows = [jnp.ones((tile_rows,), bool)] + [
        jnp.broadcast_to(ok, (HALO,)) for _, ok in row_parts
    ]
    ok_rows = jnp.concatenate(ok_rows)
    margins_k, margins_v = [], []
    oks = [jnp.ones((per_query,), bool)]
    for got, ok in row_parts:
        oks.append(jnp.broadcast_to(ok, (HALO * tile_cols,)))
    for got, ok in column_parts:
        oks.append(jnp.repeat(ok_rows & ok, HALO))
    for got, _ in row_parts + column_parts:
        margins_k.append(got[0].reshape(frames, -1, features).astype(jnp.float32))
        margins_v.append(got[1].reshape(frames, -1, features))
    margin_sq = lax.psum(
        jnp.concatenate([jnp.sum(part * part, axis=-1) for part in margins_k], axis=1), "ha"
    )
    parts_k = [normed_key.reshape(frames, -1, features)]
    at = 0
    for part in margins_k:
        parts_k.append(normed(part, margin_sq[:, at : at + part.shape[1]], key_gain))
        at += part.shape[1]
    parts_v = [values_now.reshape(frames, -1, features)] + margins_v
    bias = jnp.where(jnp.concatenate(oks), 0.0, masked_score).astype(jnp.float32)
    bias = jnp.tile(bias, frames)[None]

    flat_query = normed_query.reshape(frames, per_query, features)
    acc, ml = near_attention(flat_query, parts_k, parts_v, bias)
    padding = (-list_length) % CHUNK
    slots = jnp.pad(target, (0, padding))
    attended = far_attention(flat_query, acc, ml, far_blocks, block_counts, slots)
    return attended.reshape(frames, tile_rows, tile_cols, features)


def solution(mesh):
    return jax.shard_map(
        local,
        mesh=mesh,
        in_specs=(
            P(None, "ty", "tx", "ha"),
            P(None, "ty", "tx", "ha"),
            P(None, "ty", "tx", "ha"),
            P("ha"),
            P("ha"),
            P(("ty", "tx"), None, "ha"),
            P(("ty", "tx"), None, "ha"),
            P(("ty", "tx"), None),
            P(("ty", "tx")),
        ),
        out_specs=P(None, "ty", "tx", "ha"),
        check_vma=False,
    )
```

```python
import functools
import math

import jax
import jax.numpy as jnp
from jax import lax
from jax.experimental import pallas as pl
from jax.experimental.pallas import tpu as pltpu
from jax.sharding import PartitionSpec as P

HD = 128
HALO = 4
CHUNK = 16

epsilon = 1e-06
masked_score = -1e30
log2_scale = HD ** (-0.5) * math.log2(math.e)


def neighbours(cells, axis, dim, width):
    count = lax.axis_size(axis)
    size = cells.shape[dim]
    head = lax.slice_in_dim(cells, 0, width, axis=dim)
    tail = lax.slice_in_dim(cells, size - width, size, axis=dim)
    where_am_i = lax.axis_index(axis)
    if count == 2:
        mine = jnp.where(where_am_i == 0, tail, head)
        got = lax.ppermute(mine, axis, [(0, 1), (1, 0)])
        return [(got, jnp.bool_(True))]
    ends = count - 1
    before = lax.ppermute(tail, axis, [(i, i + 1) for i in range(ends)])
    after = lax.ppermute(head, axis, [(i + 1, i) for i in range(ends)])
    return [(before, where_am_i > 0), (after, where_am_i < ends)]


def slot_ranks(owners):
    length = owners.shape[-1]
    earlier = lax.broadcasted_iota(jnp.int32, (length, length), 1) < lax.broadcasted_iota(
        jnp.int32, (length, length), 0
    )
    same_owner = owners[..., :, None] == owners[..., None, :]
    return jnp.sum(jnp.where(same_owner & earlier, 1, 0), axis=-1).astype(jnp.int32)


def near_kernel(frames, per_query, n_parts, q_ref, bias_ref, *refs):
    parts_k = refs[:n_parts]
    parts_v = refs[n_parts : 2 * n_parts]
    acc_ref, ml_ref, kbuf, vbuf = refs[2 * n_parts :]
    span = kbuf.shape[0] // frames
    for f in range(frames):
        start = f * span
        for k_ref, v_ref in zip(parts_k, parts_v):
            rows = k_ref.shape[1]
            kbuf[start : start + rows, :] = k_ref[f]
            vbuf[start : start + rows, :HD] = v_ref[f]
            start += rows
    vbuf[:, HD:] = jnp.ones((vbuf.shape[0], HD), jnp.bfloat16)
    for f in range(frames):
        keys = (f + 1) * span
        s = lax.dot_general(
            q_ref[f], kbuf[:keys], (((1,), (1,)), ((), ())), preferred_element_type=jnp.float32
        )
        s = s + bias_ref[:, :keys]
        m = jnp.max(s, axis=1, keepdims=True) * log2_scale
        p = jnp.exp2(s * log2_scale - m).astype(jnp.bfloat16)
        o = jnp.dot(p, vbuf[:keys], preferred_element_type=jnp.float32)
        acc_ref[f] = o[:, :HD]
        lane = lax.broadcasted_iota(jnp.int32, (per_query, HD), 1)
        ml_ref[0, f] = jnp.where(lane < HD // 2, m, o[:, HD:])


def far_kernel(
    frames, per_query, tokens, count_ref, slot_ref, q_ref, acc_in, ml_in, k_ref, v_ref, out_ref,
    kbuf, vbuf, m_sc, l_sc, acc_sc,
):
    count = count_ref[0]
    vbuf[:, HD:] = jnp.ones((vbuf.shape[0], HD), jnp.bfloat16)
    for f in range(frames):
        ml = ml_in[0, f]
        m_sc[f] = jnp.broadcast_to(ml[:, :1], (per_query, HD))
        l_sc[f] = jnp.broadcast_to(ml[:, HD // 2 : HD // 2 + 1], (per_query, HD))
        acc_sc[f] = acc_in[f]

    def chunk(c, carry):
        for i in range(CHUNK):
            slot = slot_ref[c * CHUNK + i]
            kbuf[i * tokens : (i + 1) * tokens, :] = k_ref[slot, 0]
            vbuf[i * tokens : (i + 1) * tokens, :HD] = v_ref[slot, 0]
        place = lax.broadcasted_iota(jnp.int32, (1, CHUNK * tokens), 1)
        bias = jnp.where(place < (count - c * CHUNK) * tokens, 0.0, masked_score)
        for f in range(frames):
            s = lax.dot_general(
                q_ref[f], kbuf[...], (((1,), (1,)), ((), ())), preferred_element_type=jnp.float32
            )
            s = s + bias
            m_old = m_sc[f]
            m_new = jnp.maximum(m_old, jnp.max(s, axis=1, keepdims=True) * log2_scale)
            p = jnp.exp2(s * log2_scale - m_new[:, :1]).astype(jnp.bfloat16)
            o = jnp.dot(p, vbuf[...], preferred_element_type=jnp.float32)
            a = jnp.exp2(m_old - m_new)
            acc_sc[f] = acc_sc[f] * a + o[:, :HD]
            l_sc[f] = l_sc[f] * a + o[:, HD:]
            m_sc[f] = m_new
        return carry

    lax.fori_loop(0, (count + CHUNK - 1) // CHUNK, chunk, 0)
    for f in range(frames):
        out_ref[f] = (acc_sc[f] / l_sc[f]).astype(jnp.bfloat16)


def near_attention(query, parts_k, parts_v, bias):
    frames, per_query, features = query.shape
    heads = features // HD
    span = sum(part.shape[1] for part in parts_k)

    def spec(rows):
        return pl.BlockSpec((frames, rows, HD), lambda h: (0, 0, h))

    part_specs = [spec(part.shape[1]) for part in parts_k]
    keys = frames * span
    return pl.pallas_call(
        functools.partial(near_kernel, frames, per_query, len(parts_k)),
        grid=(heads,),
        in_specs=[spec(per_query), pl.BlockSpec((1, keys), lambda h: (0, 0))]
        + part_specs
        + part_specs,
        out_specs=[
            spec(per_query),
            pl.BlockSpec((1, frames, per_query, HD), lambda h: (h, 0, 0, 0)),
        ],
        out_shape=[
            jax.ShapeDtypeStruct((frames, per_query, features), jnp.float32),
            jax.ShapeDtypeStruct((heads, frames, per_query, HD), jnp.float32),
        ],
        scratch_shapes=[
            pltpu.VMEM((keys, HD), jnp.bfloat16),
            pltpu.VMEM((keys, 2 * HD), jnp.bfloat16),
        ],
        compiler_params=pltpu.CompilerParams(vmem_limit_bytes=40 << 20),
        cost_estimate=pl.CostEstimate(
            flops=heads * frames * per_query * keys * HD * 6,
            bytes_accessed=30 << 20,
            transcendentals=heads * frames * per_query * keys,
        ),
        name="near",
    )(query, bias, *parts_k, *parts_v)


def pick_kernel(total, group, wanted_ref, keys_ref, values_ref, out_ref, held, in_sem, out_sem):
    groups = total // group

    def fetch(i, carry):
        block = wanted_ref[i]
        sem = in_sem.at[i // group]
        pltpu.make_async_copy(keys_ref.at[block], held.at[i, 0], sem).start()
        pltpu.make_async_copy(values_ref.at[block], held.at[i, 1], sem).start()
        return carry

    lax.fori_loop(0, total, fetch, 0)
    for g in range(groups):
        part = pl.ds(g * group, group)
        pltpu.make_async_copy(held.at[part], held.at[part], in_sem.at[g]).wait()
        pltpu.make_async_copy(held.at[part], out_ref.at[part], out_sem.at[g]).start()
    for g in range(groups):
        part = pl.ds(g * group, group)
        pltpu.make_async_copy(held.at[part], out_ref.at[part], out_sem.at[g]).wait()


def pick_blocks(wanted, keys, values):
    total = wanted.shape[0]
    group = 8 if total % 8 == 0 else 1
    shape = (total, 2) + keys.shape[1:]
    return pl.pallas_call(
        functools.partial(pick_kernel, total, group),
        grid_spec=pltpu.PrefetchScalarGridSpec(
            num_scalar_prefetch=1,
            grid=(),
            in_specs=[pl.BlockSpec(memory_space=pl.ANY)] * 2,
            out_specs=pl.BlockSpec(memory_space=pl.ANY),
            scratch_shapes=[
                pltpu.VMEM(shape, keys.dtype),
                pltpu.SemaphoreType.DMA((total // group,)),
                pltpu.SemaphoreType.DMA((total // group,)),
            ],
        ),
        out_shape=jax.ShapeDtypeStruct(shape, keys.dtype),
        compiler_params=pltpu.CompilerParams(vmem_limit_bytes=16 << 20),
        cost_estimate=pl.CostEstimate(flops=0, bytes_accessed=20 << 20, transcendentals=0),
        name="pick",
    )(wanted, keys, values)


def far_attention(query, acc, ml, blocks, count, slots):
    frames, per_query, features = query.shape
    all_slots, _, tokens, width = blocks.shape
    heads = width // HD
    spec = pl.BlockSpec((frames, per_query, HD), lambda h, *_: (0, 0, h))
    k_spec = pl.BlockSpec((all_slots, 1, tokens, HD), lambda h, *_: (0, 0, 0, h))
    v_spec = pl.BlockSpec((all_slots, 1, tokens, HD), lambda h, *_: (0, 1, 0, h))
    return pl.pallas_call(
        functools.partial(far_kernel, frames, per_query, tokens),
        grid_spec=pltpu.PrefetchScalarGridSpec(
            num_scalar_prefetch=2,
            grid=(heads,),
            in_specs=[
                spec,
                spec,
                pl.BlockSpec((1, frames, per_query, HD), lambda h, *_: (h, 0, 0, 0)),
                k_spec,
                v_spec,
            ],
            out_specs=pl.BlockSpec((frames, per_query, HD), lambda h, *_: (0, 0, h)),
            scratch_shapes=[
                pltpu.VMEM((CHUNK * tokens, HD), jnp.bfloat16),
                pltpu.VMEM((CHUNK * tokens, 2 * HD), jnp.bfloat16),
                pltpu.VMEM((frames, per_query, HD), jnp.float32),
                pltpu.VMEM((frames, per_query, HD), jnp.float32),
                pltpu.VMEM((frames, per_query, HD), jnp.float32),
            ],
        ),
        out_shape=jax.ShapeDtypeStruct((frames, per_query, width), jnp.bfloat16),
        compiler_params=pltpu.CompilerParams(vmem_limit_bytes=40 << 20),
        cost_estimate=pl.CostEstimate(
            flops=heads * frames * per_query * 1536 * HD * 6,
            bytes_accessed=30 << 20,
            transcendentals=heads * frames * per_query * 1536,
        ),
        name="far",
    )(count, slots, query, acc, ml, blocks, blocks)


def local(
    queries,
    keys_now,
    values_now,
    query_gain,
    key_gain,
    cached_keys,
    cached_values,
    block_lists,
    block_counts,
):
    frames, tile_rows, tile_cols, features = queries.shape
    owners_all = lax.axis_size("ty") * lax.axis_size("tx")
    full_width = features * lax.axis_size("ha")
    per_query = tile_rows * tile_cols
    per_tile, block_tokens = cached_keys.shape[:2]

    listed = block_lists[0]
    list_length = listed.shape[0]
    owners = listed // per_tile
    within = listed % per_tile
    slot_rank = slot_ranks(owners)
    capacity = max(2, 4 * list_length // (3 * owners_all))
    target = owners * capacity + slot_rank
    all_slots = lax.broadcasted_iota(jnp.int32, (1, owners_all * capacity), 1)
    matches = target[:, None] == all_slots
    outgoing = jnp.sum(jnp.where(matches, within[:, None], 0), axis=0).reshape(owners_all, capacity)
    wanted = lax.all_to_all(outgoing, ("ty", "tx"), split_axis=0, concat_axis=0, tiled=True)
    wanted = wanted.reshape(-1)

    out = pick_blocks(wanted, cached_keys, cached_values)
    back = lax.all_to_all(
        out.reshape((owners_all, capacity) + out.shape[1:]),
        ("ty", "tx"),
        split_axis=0,
        concat_axis=0,
        tiled=True,
    )
    far_blocks = back.reshape((-1,) + out.shape[1:])

    now_keys, now_values, _ = lax.optimization_barrier((keys_now, values_now, wanted))
    paired = jnp.stack([now_keys, now_values])
    row_parts = neighbours(paired, "ty", 2, HALO)
    column = jnp.concatenate(
        [jnp.concatenate([part[..., :HALO, :], part[..., -HALO:, :]], axis=3) for part in
         [paired] + [got for got, _ in row_parts]],
        axis=2,
    )
    column_parts = neighbours(column, "tx", 3, HALO)

    query_wide = queries.astype(jnp.float32)
    key_wide = keys_now.astype(jnp.float32)
    query_sq, key_sq = lax.psum(
        (jnp.sum(query_wide * query_wide, axis=-1), jnp.sum(key_wide * key_wide, axis=-1)), "ha"
    )

    def normed(wide, squares, gain):
        return (wide * lax.rsqrt(squares / full_width + epsilon)[..., None] * gain).astype(
            jnp.bfloat16
        )

    normed_key = normed(key_wide, key_sq, key_gain)
    normed_query = normed(query_wide, query_sq, query_gain)

    ok_rows = [jnp.ones((tile_rows,), bool)] + [
        jnp.broadcast_to(ok, (HALO,)) for _, ok in row_parts
    ]
    ok_rows = jnp.concatenate(ok_rows)
    margins_k, margins_v = [], []
    oks = [jnp.ones((per_query,), bool)]
    for got, ok in row_parts:
        oks.append(jnp.broadcast_to(ok, (HALO * tile_cols,)))
    for got, ok in column_parts:
        oks.append(jnp.repeat(ok_rows & ok, HALO))
    for got, _ in row_parts + column_parts:
        margins_k.append(got[0].reshape(frames, -1, features).astype(jnp.float32))
        margins_v.append(got[1].reshape(frames, -1, features))
    margin_sq = lax.psum(
        jnp.concatenate([jnp.sum(part * part, axis=-1) for part in margins_k], axis=1), "ha"
    )
    parts_k = [normed_key.reshape(frames, -1, features)]
    at = 0
    for part in margins_k:
        parts_k.append(normed(part, margin_sq[:, at : at + part.shape[1]], key_gain))
        at += part.shape[1]
    parts_v = [values_now.reshape(frames, -1, features)] + margins_v
    bias = jnp.where(jnp.concatenate(oks), 0.0, masked_score).astype(jnp.float32)
    bias = jnp.tile(bias, frames)[None]

    flat_query = normed_query.reshape(frames, per_query, features)
    acc, ml = near_attention(flat_query, parts_k, parts_v, bias)
    padding = (-list_length) % CHUNK
    slots = jnp.pad(target, (0, padding))
    attended = far_attention(flat_query, acc, ml, far_blocks, block_counts, slots)
    return attended.reshape(frames, tile_rows, tile_cols, features)


def solution(mesh):
    return jax.shard_map(
        local,
        mesh=mesh,
        in_specs=(
            P(None, "ty", "tx", "ha"),
            P(None, "ty", "tx", "ha"),
            P(None, "ty", "tx", "ha"),
            P("ha"),
            P("ha"),
            P(("ty", "tx"), None, "ha"),
            P(("ty", "tx"), None, "ha"),
            P(("ty", "tx"), None),
            P(("ty", "tx")),
        ),
        out_specs=P(None, "ty", "tx", "ha"),
        check_vma=False,
    )
```

```python
import functools
import math

import jax
import jax.numpy as jnp
from jax import lax
from jax.experimental import pallas as pl
from jax.experimental.pallas import tpu as pltpu
from jax.sharding import PartitionSpec as P

HD = 128
HALO = 4
CHUNK = 16

epsilon = 1e-06
masked_score = -1e30
log2_scale = HD ** (-0.5) * math.log2(math.e)


def neighbours(cells, axis, dim, width):
    count = lax.axis_size(axis)
    size = cells.shape[dim]
    head = lax.slice_in_dim(cells, 0, width, axis=dim)
    tail = lax.slice_in_dim(cells, size - width, size, axis=dim)
    where_am_i = lax.axis_index(axis)
    if count == 2:
        mine = jnp.where(where_am_i == 0, tail, head)
        got = lax.ppermute(mine, axis, [(0, 1), (1, 0)])
        return [(got, jnp.bool_(True))]
    ends = count - 1
    before = lax.ppermute(tail, axis, [(i, i + 1) for i in range(ends)])
    after = lax.ppermute(head, axis, [(i + 1, i) for i in range(ends)])
    return [(before, where_am_i > 0), (after, where_am_i < ends)]


def slot_ranks(owners):
    length = owners.shape[-1]
    earlier = lax.broadcasted_iota(jnp.int32, (length, length), 1) < lax.broadcasted_iota(
        jnp.int32, (length, length), 0
    )
    same_owner = owners[..., :, None] == owners[..., None, :]
    return jnp.sum(jnp.where(same_owner & earlier, 1, 0), axis=-1).astype(jnp.int32)


def near_kernel(frames, per_query, n_parts, q_ref, bias_ref, *refs):
    parts_k = refs[:n_parts]
    parts_v = refs[n_parts : 2 * n_parts]
    acc_ref, ml_ref, kbuf, vbuf = refs[2 * n_parts :]
    span = kbuf.shape[0] // frames
    for f in range(frames):
        start = f * span
        for k_ref, v_ref in zip(parts_k, parts_v):
            rows = k_ref.shape[1]
            kbuf[start : start + rows, :] = k_ref[f]
            vbuf[start : start + rows, :HD] = v_ref[f]
            start += rows
    vbuf[:, HD:] = jnp.ones((vbuf.shape[0], HD), jnp.bfloat16)
    for f in range(frames):
        keys = (f + 1) * span
        s = lax.dot_general(
            q_ref[f], kbuf[:keys], (((1,), (1,)), ((), ())), preferred_element_type=jnp.float32
        )
        s = s + bias_ref[:, :keys]
        m = jnp.max(s, axis=1, keepdims=True) * log2_scale
        p = jnp.exp2(s * log2_scale - m).astype(jnp.bfloat16)
        o = jnp.dot(p, vbuf[:keys], preferred_element_type=jnp.float32)
        acc_ref[f] = o[:, :HD]
        lane = lax.broadcasted_iota(jnp.int32, (per_query, HD), 1)
        ml_ref[0, f] = jnp.where(lane < HD // 2, m, o[:, HD:])


def far_kernel(
    frames, per_query, tokens, count_ref, slot_ref, q_ref, acc_in, ml_in, k_ref, v_ref, out_ref,
    kbuf, vbuf, m_sc, l_sc, acc_sc,
):
    count = count_ref[0]
    vbuf[:, HD:] = jnp.ones((vbuf.shape[0], HD), jnp.bfloat16)
    for f in range(frames):
        ml = ml_in[0, f]
        m_sc[f] = jnp.broadcast_to(ml[:, :1], (per_query, HD))
        l_sc[f] = jnp.broadcast_to(ml[:, HD // 2 : HD // 2 + 1], (per_query, HD))
        acc_sc[f] = acc_in[f]

    def chunk(c, carry):
        for i in range(CHUNK):
            slot = slot_ref[c * CHUNK + i]
            kbuf[i * tokens : (i + 1) * tokens, :] = k_ref[slot, 0]
            vbuf[i * tokens : (i + 1) * tokens, :HD] = v_ref[slot, 0]
        place = lax.broadcasted_iota(jnp.int32, (1, CHUNK * tokens), 1)
        bias = jnp.where(place < (count - c * CHUNK) * tokens, 0.0, masked_score)
        for f in range(frames):
            s = lax.dot_general(
                q_ref[f], kbuf[...], (((1,), (1,)), ((), ())), preferred_element_type=jnp.float32
            )
            s = s + bias
            m_old = m_sc[f]
            m_new = jnp.maximum(m_old, jnp.max(s, axis=1, keepdims=True) * log2_scale)
            p = jnp.exp2(s * log2_scale - m_new[:, :1]).astype(jnp.bfloat16)
            o = jnp.dot(p, vbuf[...], preferred_element_type=jnp.float32)
            a = jnp.exp2(m_old - m_new)
            acc_sc[f] = acc_sc[f] * a + o[:, :HD]
            l_sc[f] = l_sc[f] * a + o[:, HD:]
            m_sc[f] = m_new
        return carry

    lax.fori_loop(0, (count + CHUNK - 1) // CHUNK, chunk, 0)
    for f in range(frames):
        out_ref[f] = (acc_sc[f] / l_sc[f]).astype(jnp.bfloat16)


def near_attention(query, parts_k, parts_v, bias):
    frames, per_query, features = query.shape
    heads = features // HD
    span = sum(part.shape[1] for part in parts_k)

    def spec(rows):
        return pl.BlockSpec((frames, rows, HD), lambda h: (0, 0, h))

    part_specs = [spec(part.shape[1]) for part in parts_k]
    keys = frames * span
    return pl.pallas_call(
        functools.partial(near_kernel, frames, per_query, len(parts_k)),
        grid=(heads,),
        in_specs=[spec(per_query), pl.BlockSpec((1, keys), lambda h: (0, 0))]
        + part_specs
        + part_specs,
        out_specs=[
            spec(per_query),
            pl.BlockSpec((1, frames, per_query, HD), lambda h: (h, 0, 0, 0)),
        ],
        out_shape=[
            jax.ShapeDtypeStruct((frames, per_query, features), jnp.float32),
            jax.ShapeDtypeStruct((heads, frames, per_query, HD), jnp.float32),
        ],
        scratch_shapes=[
            pltpu.VMEM((keys, HD), jnp.bfloat16),
            pltpu.VMEM((keys, 2 * HD), jnp.bfloat16),
        ],
        compiler_params=pltpu.CompilerParams(vmem_limit_bytes=60 << 20),
        cost_estimate=pl.CostEstimate(
            flops=heads * frames * per_query * keys * HD * 6,
            bytes_accessed=30 << 20,
            transcendentals=heads * frames * per_query * keys,
        ),
        name="near",
    )(query, bias, *parts_k, *parts_v)


def pick_kernel(total, group, wanted_ref, keys_ref, values_ref, out_ref, held, in_sem, out_sem):
    groups = total // group

    def fetch(i, carry):
        block = wanted_ref[i]
        sem = in_sem.at[i // group]
        pltpu.make_async_copy(keys_ref.at[block], held.at[i, 0], sem).start()
        pltpu.make_async_copy(values_ref.at[block], held.at[i, 1], sem).start()
        return carry

    lax.fori_loop(0, total, fetch, 0)
    for g in range(groups):
        part = pl.ds(g * group, group)
        pltpu.make_async_copy(held.at[part], held.at[part], in_sem.at[g]).wait()
        pltpu.make_async_copy(held.at[part], out_ref.at[part], out_sem.at[g]).start()
    for g in range(groups):
        part = pl.ds(g * group, group)
        pltpu.make_async_copy(held.at[part], out_ref.at[part], out_sem.at[g]).wait()


def pick_blocks(wanted, keys, values):
    total = wanted.shape[0]
    group = 8 if total % 8 == 0 else 1
    shape = (total, 2) + keys.shape[1:]
    return pl.pallas_call(
        functools.partial(pick_kernel, total, group),
        grid_spec=pltpu.PrefetchScalarGridSpec(
            num_scalar_prefetch=1,
            grid=(),
            in_specs=[pl.BlockSpec(memory_space=pl.ANY)] * 2,
            out_specs=pl.BlockSpec(memory_space=pl.ANY),
            scratch_shapes=[
                pltpu.VMEM(shape, keys.dtype),
                pltpu.SemaphoreType.DMA((total // group,)),
                pltpu.SemaphoreType.DMA((total // group,)),
            ],
        ),
        out_shape=jax.ShapeDtypeStruct(shape, keys.dtype),
        compiler_params=pltpu.CompilerParams(vmem_limit_bytes=60 << 20),
        cost_estimate=pl.CostEstimate(flops=0, bytes_accessed=20 << 20, transcendentals=0),
        name="pick",
    )(wanted, keys, values)


def far_attention(query, acc, ml, blocks, count, slots):
    frames, per_query, features = query.shape
    all_slots, _, tokens, width = blocks.shape
    heads = width // HD
    spec = pl.BlockSpec((frames, per_query, HD), lambda h, *_: (0, 0, h))
    k_spec = pl.BlockSpec((all_slots, 1, tokens, HD), lambda h, *_: (0, 0, 0, h))
    v_spec = pl.BlockSpec((all_slots, 1, tokens, HD), lambda h, *_: (0, 1, 0, h))
    return pl.pallas_call(
        functools.partial(far_kernel, frames, per_query, tokens),
        grid_spec=pltpu.PrefetchScalarGridSpec(
            num_scalar_prefetch=2,
            grid=(heads,),
            in_specs=[
                spec,
                spec,
                pl.BlockSpec((1, frames, per_query, HD), lambda h, *_: (h, 0, 0, 0)),
                k_spec,
                v_spec,
            ],
            out_specs=pl.BlockSpec((frames, per_query, HD), lambda h, *_: (0, 0, h)),
            scratch_shapes=[
                pltpu.VMEM((CHUNK * tokens, HD), jnp.bfloat16),
                pltpu.VMEM((CHUNK * tokens, 2 * HD), jnp.bfloat16),
                pltpu.VMEM((frames, per_query, HD), jnp.float32),
                pltpu.VMEM((frames, per_query, HD), jnp.float32),
                pltpu.VMEM((frames, per_query, HD), jnp.float32),
            ],
        ),
        out_shape=jax.ShapeDtypeStruct((frames, per_query, width), jnp.bfloat16),
        compiler_params=pltpu.CompilerParams(vmem_limit_bytes=60 << 20),
        cost_estimate=pl.CostEstimate(
            flops=heads * frames * per_query * 1536 * HD * 6,
            bytes_accessed=30 << 20,
            transcendentals=heads * frames * per_query * 1536,
        ),
        name="far",
    )(count, slots, query, acc, ml, blocks, blocks)


def local(
    queries,
    keys_now,
    values_now,
    query_gain,
    key_gain,
    cached_keys,
    cached_values,
    block_lists,
    block_counts,
):
    frames, tile_rows, tile_cols, features = queries.shape
    owners_all = lax.axis_size("ty") * lax.axis_size("tx")
    full_width = features * lax.axis_size("ha")
    per_query = tile_rows * tile_cols
    per_tile, block_tokens = cached_keys.shape[:2]

    listed = block_lists[0]
    list_length = listed.shape[0]
    owners = listed // per_tile
    within = listed % per_tile
    slot_rank = slot_ranks(owners)
    capacity = max(2, 4 * list_length // (3 * owners_all))
    target = owners * capacity + slot_rank
    all_slots = lax.broadcasted_iota(jnp.int32, (1, owners_all * capacity), 1)
    matches = target[:, None] == all_slots
    outgoing = jnp.sum(jnp.where(matches, within[:, None], 0), axis=0).reshape(owners_all, capacity)
    wanted = lax.all_to_all(outgoing, ("ty", "tx"), split_axis=0, concat_axis=0, tiled=True)
    wanted = wanted.reshape(-1)

    out = pick_blocks(wanted, cached_keys, cached_values)
    now_keys, now_values, _ = lax.optimization_barrier((keys_now, values_now, wanted))
    paired = jnp.stack([now_keys, now_values])
    row_parts = neighbours(paired, "ty", 2, HALO)
    out, row_got = lax.optimization_barrier((out, [got for got, _ in row_parts]))
    row_parts = [(got, ok) for got, (_, ok) in zip(row_got, row_parts)]
    back = lax.all_to_all(
        out.reshape((owners_all, capacity) + out.shape[1:]),
        ("ty", "tx"),
        split_axis=0,
        concat_axis=0,
        tiled=True,
    )
    far_blocks = back.reshape((-1,) + out.shape[1:])
    column = jnp.concatenate(
        [jnp.concatenate([part[..., :HALO, :], part[..., -HALO:, :]], axis=3) for part in
         [paired] + [got for got, _ in row_parts]],
        axis=2,
    )
    column_parts = neighbours(column, "tx", 3, HALO)

    query_wide = queries.astype(jnp.float32)
    key_wide = keys_now.astype(jnp.float32)
    query_sq, key_sq = lax.psum(
        (jnp.sum(query_wide * query_wide, axis=-1), jnp.sum(key_wide * key_wide, axis=-1)), "ha"
    )

    def normed(wide, squares, gain):
        return (wide * lax.rsqrt(squares / full_width + epsilon)[..., None] * gain).astype(
            jnp.bfloat16
        )

    normed_key = normed(key_wide, key_sq, key_gain)
    normed_query = normed(query_wide, query_sq, query_gain)

    ok_rows = [jnp.ones((tile_rows,), bool)] + [
        jnp.broadcast_to(ok, (HALO,)) for _, ok in row_parts
    ]
    ok_rows = jnp.concatenate(ok_rows)
    margins_k, margins_v = [], []
    oks = [jnp.ones((per_query,), bool)]
    for got, ok in row_parts:
        oks.append(jnp.broadcast_to(ok, (HALO * tile_cols,)))
    for got, ok in column_parts:
        oks.append(jnp.repeat(ok_rows & ok, HALO))
    for got, _ in row_parts + column_parts:
        margins_k.append(got[0].reshape(frames, -1, features).astype(jnp.float32))
        margins_v.append(got[1].reshape(frames, -1, features))
    margin_sq = lax.psum(
        jnp.concatenate([jnp.sum(part * part, axis=-1) for part in margins_k], axis=1), "ha"
    )
    parts_k = [normed_key.reshape(frames, -1, features)]
    at = 0
    for part in margins_k:
        parts_k.append(normed(part, margin_sq[:, at : at + part.shape[1]], key_gain))
        at += part.shape[1]
    parts_v = [values_now.reshape(frames, -1, features)] + margins_v
    bias = jnp.where(jnp.concatenate(oks), 0.0, masked_score).astype(jnp.float32)
    bias = jnp.tile(bias, frames)[None]

    flat_query = normed_query.reshape(frames, per_query, features)
    acc, ml = near_attention(flat_query, parts_k, parts_v, bias)
    padding = (-list_length) % CHUNK
    slots = jnp.pad(target, (0, padding))
    attended = far_attention(flat_query, acc, ml, far_blocks, block_counts, slots)
    return attended.reshape(frames, tile_rows, tile_cols, features)


def solution(mesh):
    return jax.shard_map(
        local,
        mesh=mesh,
        in_specs=(
            P(None, "ty", "tx", "ha"),
            P(None, "ty", "tx", "ha"),
            P(None, "ty", "tx", "ha"),
            P("ha"),
            P("ha"),
            P(("ty", "tx"), None, "ha"),
            P(("ty", "tx"), None, "ha"),
            P(("ty", "tx"), None),
            P(("ty", "tx")),
        ),
        out_specs=P(None, "ty", "tx", "ha"),
        check_vma=False,
    )
```

```python
import functools
import math

import jax
import jax.numpy as jnp
from jax import lax
from jax.experimental import pallas as pl
from jax.experimental.pallas import tpu as pltpu
from jax.sharding import PartitionSpec as P

HD = 128
HALO = 4
CHUNK = 16

epsilon = 1e-06
masked_score = -1e30
log2_scale = HD ** (-0.5) * math.log2(math.e)


def neighbours(cells, axis, dim, width):
    count = lax.axis_size(axis)
    size = cells.shape[dim]
    head = lax.slice_in_dim(cells, 0, width, axis=dim)
    tail = lax.slice_in_dim(cells, size - width, size, axis=dim)
    where_am_i = lax.axis_index(axis)
    if count == 2:
        mine = jnp.where(where_am_i == 0, tail, head)
        got = lax.ppermute(mine, axis, [(0, 1), (1, 0)])
        return [(got, jnp.bool_(True))]
    ends = count - 1
    before = lax.ppermute(tail, axis, [(i, i + 1) for i in range(ends)])
    after = lax.ppermute(head, axis, [(i + 1, i) for i in range(ends)])
    return [(before, where_am_i > 0), (after, where_am_i < ends)]


def slot_ranks(owners):
    length = owners.shape[-1]
    earlier = lax.broadcasted_iota(jnp.int32, (length, length), 1) < lax.broadcasted_iota(
        jnp.int32, (length, length), 0
    )
    same_owner = owners[..., :, None] == owners[..., None, :]
    return jnp.sum(jnp.where(same_owner & earlier, 1, 0), axis=-1).astype(jnp.int32)


def near_kernel(frames, per_query, n_parts, q_ref, bias_ref, *refs):
    parts_k = refs[:n_parts]
    parts_v = refs[n_parts : 2 * n_parts]
    acc_ref, ml_ref, kbuf, vbuf = refs[2 * n_parts :]
    span = kbuf.shape[0] // frames
    for f in range(frames):
        start = f * span
        for k_ref, v_ref in zip(parts_k, parts_v):
            rows = k_ref.shape[1]
            kbuf[start : start + rows, :] = k_ref[f]
            vbuf[start : start + rows, :HD] = v_ref[f]
            start += rows
    vbuf[:, HD:] = jnp.ones((vbuf.shape[0], HD), jnp.bfloat16)
    for f in range(frames):
        keys = (f + 1) * span
        s = lax.dot_general(
            q_ref[f], kbuf[:keys], (((1,), (1,)), ((), ())), preferred_element_type=jnp.float32
        )
        s = s + bias_ref[:, :keys]
        m = jnp.max(s, axis=1, keepdims=True) * log2_scale
        p = jnp.exp2(s * log2_scale - m).astype(jnp.bfloat16)
        o = jnp.dot(p, vbuf[:keys], preferred_element_type=jnp.float32)
        acc_ref[f] = o[:, :HD]
        lane = lax.broadcasted_iota(jnp.int32, (per_query, HD), 1)
        ml_ref[0, f] = jnp.where(lane < HD // 2, m, o[:, HD:])


def far_kernel(
    frames, per_query, tokens, count_ref, slot_ref, q_ref, acc_in, ml_in, k_ref, v_ref, out_ref,
    kbuf, vbuf, m_sc, l_sc, acc_sc,
):
    count = count_ref[0]
    vbuf[:, HD:] = jnp.ones((vbuf.shape[0], HD), jnp.bfloat16)
    for f in range(frames):
        ml = ml_in[0, f]
        m_sc[f] = jnp.broadcast_to(ml[:, :1], (per_query, HD))
        l_sc[f] = jnp.broadcast_to(ml[:, HD // 2 : HD // 2 + 1], (per_query, HD))
        acc_sc[f] = acc_in[f]

    def chunk(c, carry):
        for i in range(CHUNK):
            slot = slot_ref[c * CHUNK + i]
            kbuf[i * tokens : (i + 1) * tokens, :] = k_ref[slot, 0]
            vbuf[i * tokens : (i + 1) * tokens, :HD] = v_ref[slot, 0]
        place = lax.broadcasted_iota(jnp.int32, (1, CHUNK * tokens), 1)
        bias = jnp.where(place < (count - c * CHUNK) * tokens, 0.0, masked_score)
        for f in range(frames):
            s = lax.dot_general(
                q_ref[f], kbuf[...], (((1,), (1,)), ((), ())), preferred_element_type=jnp.float32
            )
            s = s + bias
            m_old = m_sc[f]
            m_new = jnp.maximum(m_old, jnp.max(s, axis=1, keepdims=True) * log2_scale)
            p = jnp.exp2(s * log2_scale - m_new[:, :1]).astype(jnp.bfloat16)
            o = jnp.dot(p, vbuf[...], preferred_element_type=jnp.float32)
            a = jnp.exp2(m_old - m_new)
            acc_sc[f] = acc_sc[f] * a + o[:, :HD]
            l_sc[f] = l_sc[f] * a + o[:, HD:]
            m_sc[f] = m_new
        return carry

    lax.fori_loop(0, (count + CHUNK - 1) // CHUNK, chunk, 0)
    for f in range(frames):
        out_ref[f] = (acc_sc[f] / l_sc[f]).astype(jnp.bfloat16)


def near_attention(query, parts_k, parts_v, bias):
    frames, per_query, features = query.shape
    heads = features // HD
    span = sum(part.shape[1] for part in parts_k)

    def spec(rows):
        return pl.BlockSpec((frames, rows, HD), lambda h: (0, 0, h))

    part_specs = [spec(part.shape[1]) for part in parts_k]
    keys = frames * span
    return pl.pallas_call(
        functools.partial(near_kernel, frames, per_query, len(parts_k)),
        grid=(heads,),
        in_specs=[spec(per_query), pl.BlockSpec((1, keys), lambda h: (0, 0))]
        + part_specs
        + part_specs,
        out_specs=[
            spec(per_query),
            pl.BlockSpec((1, frames, per_query, HD), lambda h: (h, 0, 0, 0)),
        ],
        out_shape=[
            jax.ShapeDtypeStruct((frames, per_query, features), jnp.float32),
            jax.ShapeDtypeStruct((heads, frames, per_query, HD), jnp.float32),
        ],
        scratch_shapes=[
            pltpu.VMEM((keys, HD), jnp.bfloat16),
            pltpu.VMEM((keys, 2 * HD), jnp.bfloat16),
        ],
        compiler_params=pltpu.CompilerParams(vmem_limit_bytes=60 << 20),
        cost_estimate=pl.CostEstimate(
            flops=heads * frames * per_query * keys * HD * 6,
            bytes_accessed=30 << 20,
            transcendentals=heads * frames * per_query * keys,
        ),
        name="near",
    )(query, bias, *parts_k, *parts_v)


def pick_kernel(total, group, wanted_ref, keys_ref, values_ref, out_ref, held, in_sem, out_sem):
    groups = total // group

    def fetch(i, carry):
        block = wanted_ref[i]
        sem = in_sem.at[i // group]
        pltpu.make_async_copy(keys_ref.at[block], held.at[i, 0], sem).start()
        pltpu.make_async_copy(values_ref.at[block], held.at[i, 1], sem).start()
        return carry

    lax.fori_loop(0, total, fetch, 0)
    for g in range(groups):
        part = pl.ds(g * group, group)
        pltpu.make_async_copy(held.at[part], held.at[part], in_sem.at[g]).wait()
        pltpu.make_async_copy(held.at[part], out_ref.at[part], out_sem.at[g]).start()
    for g in range(groups):
        part = pl.ds(g * group, group)
        pltpu.make_async_copy(held.at[part], out_ref.at[part], out_sem.at[g]).wait()


def pick_blocks(wanted, keys, values):
    total = wanted.shape[0]
    group = 8 if total % 8 == 0 else 1
    shape = (total, 2) + keys.shape[1:]
    return pl.pallas_call(
        functools.partial(pick_kernel, total, group),
        grid_spec=pltpu.PrefetchScalarGridSpec(
            num_scalar_prefetch=1,
            grid=(),
            in_specs=[pl.BlockSpec(memory_space=pl.ANY)] * 2,
            out_specs=pl.BlockSpec(memory_space=pl.ANY),
            scratch_shapes=[
                pltpu.VMEM(shape, keys.dtype),
                pltpu.SemaphoreType.DMA((total // group,)),
                pltpu.SemaphoreType.DMA((total // group,)),
            ],
        ),
        out_shape=jax.ShapeDtypeStruct(shape, keys.dtype),
        compiler_params=pltpu.CompilerParams(vmem_limit_bytes=60 << 20),
        cost_estimate=pl.CostEstimate(flops=0, bytes_accessed=20 << 20, transcendentals=0),
        name="pick",
    )(wanted, keys, values)


def far_attention(query, acc, ml, blocks, count, slots):
    frames, per_query, features = query.shape
    all_slots, _, tokens, width = blocks.shape
    heads = width // HD
    spec = pl.BlockSpec((frames, per_query, HD), lambda h, *_: (0, 0, h))
    k_spec = pl.BlockSpec((all_slots, 1, tokens, HD), lambda h, *_: (0, 0, 0, h))
    v_spec = pl.BlockSpec((all_slots, 1, tokens, HD), lambda h, *_: (0, 1, 0, h))
    return pl.pallas_call(
        functools.partial(far_kernel, frames, per_query, tokens),
        grid_spec=pltpu.PrefetchScalarGridSpec(
            num_scalar_prefetch=2,
            grid=(heads,),
            in_specs=[
                spec,
                spec,
                pl.BlockSpec((1, frames, per_query, HD), lambda h, *_: (h, 0, 0, 0)),
                k_spec,
                v_spec,
            ],
            out_specs=pl.BlockSpec((frames, per_query, HD), lambda h, *_: (0, 0, h)),
            scratch_shapes=[
                pltpu.VMEM((CHUNK * tokens, HD), jnp.bfloat16),
                pltpu.VMEM((CHUNK * tokens, 2 * HD), jnp.bfloat16),
                pltpu.VMEM((frames, per_query, HD), jnp.float32),
                pltpu.VMEM((frames, per_query, HD), jnp.float32),
                pltpu.VMEM((frames, per_query, HD), jnp.float32),
            ],
        ),
        out_shape=jax.ShapeDtypeStruct((frames, per_query, width), jnp.bfloat16),
        compiler_params=pltpu.CompilerParams(vmem_limit_bytes=60 << 20),
        cost_estimate=pl.CostEstimate(
            flops=heads * frames * per_query * 1536 * HD * 6,
            bytes_accessed=30 << 20,
            transcendentals=heads * frames * per_query * 1536,
        ),
        name="far",
    )(count, slots, query, acc, ml, blocks, blocks)


def local(
    queries,
    keys_now,
    values_now,
    query_gain,
    key_gain,
    cached_keys,
    cached_values,
    block_lists,
    block_counts,
):
    frames, tile_rows, tile_cols, features = queries.shape
    owners_all = lax.axis_size("ty") * lax.axis_size("tx")
    full_width = features * lax.axis_size("ha")
    per_query = tile_rows * tile_cols
    per_tile, block_tokens = cached_keys.shape[:2]

    listed = block_lists[0]
    list_length = listed.shape[0]
    owners = listed // per_tile
    within = listed % per_tile
    slot_rank = slot_ranks(owners)
    capacity = max(2, 4 * list_length // (3 * owners_all))
    target = owners * capacity + slot_rank
    all_slots = lax.broadcasted_iota(jnp.int32, (1, owners_all * capacity), 1)
    matches = target[:, None] == all_slots
    outgoing = jnp.sum(jnp.where(matches, within[:, None], 0), axis=0).reshape(owners_all, capacity)
    wanted = lax.all_to_all(outgoing, ("ty", "tx"), split_axis=0, concat_axis=0, tiled=True)
    wanted = wanted.reshape(-1)

    out = pick_blocks(wanted, cached_keys, cached_values)
    now_keys, now_values, _ = lax.optimization_barrier((keys_now, values_now, wanted))
    paired = jnp.stack([now_keys, now_values])
    row_parts = neighbours(paired, "ty", 2, HALO)
    column = jnp.concatenate(
        [jnp.concatenate([part[..., :HALO, :], part[..., -HALO:, :]], axis=3) for part in
         [paired] + [got for got, _ in row_parts]],
        axis=2,
    )
    column_parts = neighbours(column, "tx", 3, HALO)
    out, column_got = lax.optimization_barrier((out, [got for got, _ in column_parts]))
    column_parts = [(got, ok) for got, (_, ok) in zip(column_got, column_parts)]
    back = lax.all_to_all(
        out.reshape((owners_all, capacity) + out.shape[1:]),
        ("ty", "tx"),
        split_axis=0,
        concat_axis=0,
        tiled=True,
    )
    far_blocks = back.reshape((-1,) + out.shape[1:])

    query_wide = queries.astype(jnp.float32)
    key_wide = keys_now.astype(jnp.float32)
    query_sq, key_sq = lax.psum(
        (jnp.sum(query_wide * query_wide, axis=-1), jnp.sum(key_wide * key_wide, axis=-1)), "ha"
    )

    def normed(wide, squares, gain):
        return (wide * lax.rsqrt(squares / full_width + epsilon)[..., None] * gain).astype(
            jnp.bfloat16
        )

    normed_key = normed(key_wide, key_sq, key_gain)
    normed_query = normed(query_wide, query_sq, query_gain)

    ok_rows = [jnp.ones((tile_rows,), bool)] + [
        jnp.broadcast_to(ok, (HALO,)) for _, ok in row_parts
    ]
    ok_rows = jnp.concatenate(ok_rows)
    margins_k, margins_v = [], []
    oks = [jnp.ones((per_query,), bool)]
    for got, ok in row_parts:
        oks.append(jnp.broadcast_to(ok, (HALO * tile_cols,)))
    for got, ok in column_parts:
        oks.append(jnp.repeat(ok_rows & ok, HALO))
    for got, _ in row_parts + column_parts:
        margins_k.append(got[0].reshape(frames, -1, features).astype(jnp.float32))
        margins_v.append(got[1].reshape(frames, -1, features))
    margin_sq = lax.psum(
        jnp.concatenate([jnp.sum(part * part, axis=-1) for part in margins_k], axis=1), "ha"
    )
    parts_k = [normed_key.reshape(frames, -1, features)]
    at = 0
    for part in margins_k:
        parts_k.append(normed(part, margin_sq[:, at : at + part.shape[1]], key_gain))
        at += part.shape[1]
    parts_v = [values_now.reshape(frames, -1, features)] + margins_v
    bias = jnp.where(jnp.concatenate(oks), 0.0, masked_score).astype(jnp.float32)
    bias = jnp.tile(bias, frames)[None]

    flat_query = normed_query.reshape(frames, per_query, features)
    acc, ml = near_attention(flat_query, parts_k, parts_v, bias)
    padding = (-list_length) % CHUNK
    slots = jnp.pad(target, (0, padding))
    attended = far_attention(flat_query, acc, ml, far_blocks, block_counts, slots)
    return attended.reshape(frames, tile_rows, tile_cols, features)


def solution(mesh):
    return jax.shard_map(
        local,
        mesh=mesh,
        in_specs=(
            P(None, "ty", "tx", "ha"),
            P(None, "ty", "tx", "ha"),
            P(None, "ty", "tx", "ha"),
            P("ha"),
            P("ha"),
            P(("ty", "tx"), None, "ha"),
            P(("ty", "tx"), None, "ha"),
            P(("ty", "tx"), None),
            P(("ty", "tx")),
        ),
        out_specs=P(None, "ty", "tx", "ha"),
        check_vma=False,
    )
```
